32 devices in a mesh: groups: 2 (over x), ctx: 16 (over z, y, core).
Axes of the slice: x: 2, y: 2, z: 4, core: 2. Of those that a mesh axis runs over, the one named last changes fastest.
Arguments:
- hidden_in: bfloat16 [4096, 2048], P(('groups', 'ctx')), parts along dimension 0, may hold values from -6 to 6
- span_order: int32 [32, 2], P('groups'), parts along dimension 0, may hold values from 0 to 31, as said below
- norm_gain: float32 [2048], replicated, may hold values from 0.5 to 1.5
- w_query: bfloat16 [2048, 2048], replicated, may hold values from -0.125 to 0.125
- w_key: bfloat16 [2048, 256], replicated, may hold values from -0.125 to 0.125
- w_value: bfloat16 [2048, 256], replicated, may hold values from -0.125 to 0.125
- query_gain: float32 [128], replicated, may hold values from 1.5 to 7
- key_gain: float32 [128], replicated, may hold values from 1.5 to 7
Outputs:
- attended: bfloat16 [4096, 2048], P(('groups', 'ctx')), parts along dimension 0
The draws below stay inside these ranges and needn't reach their ends.
There are 2 independent parts, one for each index of `groups`. The reference program is written for one: setup_inputs(seed, part) draws one part's arguments, and reference() takes and returns one part's arrays. A program takes and returns all parts, laid end to end along the dimension named above; an argument that names none is the same for every part. Nothing has to cross between parts.
Inputs may be any that keep to these rules, and one draw needn't show every extreme that they name: `span_order`: row d holds a span c and the span 2 * 16 - 1 - c with c < 16; the rows together name every span once; a device's first 64 rows are its column 0 span.
All inputs are finite; a program needn't handle non-finite values.
Results may differ from the reference program's by a relative error of at most 0.0075.
The reference program's roundings to bfloat16 on the way count: a program that leaves them out, or rounds other values in their place, can miss the bound.
Values may be sent and summed in bfloat16 or wider, within the bound.
No kernel may reach another device: no remote copies, remote signals or barrier semaphores. Data moves between devices by JAX's collectives and lax.ppermute only.
A program may use at most 128 MiB of HBM per device.

```python
import math
import jax
import jax.numpy as jnp
from jax import lax

D = 2048
HEADS = 16
KV_HEADS = 2
HEAD = 128
TOKENS = 2048
N_CTX = 16


def draw_span_order(key, part):
    shuffled = jax.random.permutation(jax.random.fold_in(key, 11), N_CTX).astype(jnp.int32)
    return jnp.stack([shuffled, 2 * N_CTX - 1 - shuffled], axis=1)


def draw_query_gain(key, part):
    subkey = jax.random.fold_in(key, 23)
    return jax.random.uniform(subkey, (HEAD,), jnp.float32, 1.5, 3.0)


def draw_key_gain(key, part):
    subkey = jax.random.fold_in(key, 37)
    return jax.random.uniform(subkey, (HEAD,), jnp.float32, 1.5, 3.0)


def block_levels(stream_key, extent, split, least, top_value):
    def one(dim, parts):
        steps = jax.random.uniform(jax.random.fold_in(jax.random.fold_in(stream_key, 6), dim), (parts,), jnp.float32, least / len(split), top_value / len(split))
        return jnp.repeat(jnp.exp(steps), extent[dim] // parts).reshape((-1,) + (1,) * (len(extent) - dim - 1))

    loudness = one(*split[0])
    for cut in split[1:]:
        loudness = loudness * one(*cut)
    return loudness


def noise(rng, shape, deviation, limit, cuts=(), held_as=jnp.bfloat16):
    array = deviation * jax.random.normal(rng, shape, jnp.float32)
    if cuts:
        array = array * block_levels(rng, shape, cuts, -0.22, 0.18)
    return jnp.clip(array, -limit, limit).astype(held_as)


def setup_inputs(seed: int = 0, part: int = 0) -> dict:
    key_of = jax.random.split(jax.random.key(seed), 9)
    part_keys = jax.random.split(jax.random.fold_in(key_of[8], part), 9)
    return {
        "hidden_in": noise(part_keys[0], (TOKENS, D), 1.0, 6.0, ((0, 16),)),
        "span_order": draw_span_order(jax.random.fold_in(jax.random.fold_in(key_of[8], part), 71), part),
        "norm_gain": jnp.clip(1.0 + 0.1 * jax.random.normal(key_of[2], (D,), jnp.float32), 0.5, 1.5),
        "w_query": noise(key_of[3], (D, HEADS * HEAD), D ** -0.5, 0.125),
        "w_key": noise(key_of[4], (D, KV_HEADS * HEAD), D ** -0.5, 0.125),
        "w_value": noise(key_of[5], (D, KV_HEADS * HEAD), D ** -0.5, 0.125),
        "query_gain": draw_query_gain(jax.random.fold_in(key_of[8], 71), part),
        "key_gain": draw_key_gain(jax.random.fold_in(key_of[8], 71), part),
    }


EPSILON = 1e-06
THETA = 1000000.0

def scaled(entries, gains):
    mean_square = lax.optimization_barrier(jnp.mean(entries * entries, axis=-1, keepdims=True))
    return entries * lax.rsqrt(mean_square + EPSILON) * gains

def rotated(entries, position):
    head_width = entries.shape[-1]
    halfway = head_width // 2
    exponent = jnp.arange(halfway, dtype=jnp.float32) * (2.0 / head_width)
    inverse = jnp.power(jnp.float32(THETA), -exponent)
    angles = position.astype(jnp.float32)[:, None] * inverse[None, :]
    cosine = jnp.cos(angles)[:, None, :]
    sine_part = jnp.sin(angles)[:, None, :]
    first_half = entries[..., :halfway]
    second = entries[..., halfway:]
    return jnp.concatenate([first_half * cosine - second * sine_part, second * cosine + first_half * sine_part], axis=-1)

def project(hidden_in, norm_gain, w_query, w_key, w_value, query_gain, key_gain, position):
    row_count = hidden_in.shape[0]
    normed = scaled(hidden_in.astype(jnp.float32), norm_gain).astype(jnp.bfloat16)
    queries = jnp.dot(normed, w_query, preferred_element_type=jnp.float32).reshape(row_count, HEADS, HEAD)
    queries = rotated(scaled(queries, query_gain), position).astype(jnp.bfloat16)
    key_heads = jnp.dot(normed, w_key, preferred_element_type=jnp.float32).reshape(row_count, KV_HEADS, HEAD)
    key_heads = rotated(scaled(key_heads, key_gain), position).astype(jnp.bfloat16)
    values = jnp.dot(normed, w_value, preferred_element_type=jnp.float32).astype(jnp.bfloat16)
    return (queries, key_heads, values)

def reference(hidden_in, span_order, norm_gain, w_query, w_key, w_value, query_gain, key_gain):
    row_count = hidden_in.shape[0]
    tok_rows = row_count // N_CTX
    half_rows = tok_rows // 2
    row_index = jnp.arange(row_count, dtype=jnp.int32)
    device = row_index // tok_rows
    within = row_index % tok_rows
    span_ids = span_order[device, within // half_rows]
    position = (span_ids * half_rows + within % half_rows).astype(jnp.int32)
    queries, key_heads, values = project(hidden_in, norm_gain, w_query, w_key, w_value, query_gain, key_gain, position)
    group_size = HEADS // KV_HEADS
    block_rows = math.gcd(row_count, 256)
    keys_wide = key_heads.astype(jnp.float32)
    values_wide = values.reshape(row_count, KV_HEADS, HEAD).astype(jnp.float32)
    query_blocks = queries.reshape(row_count // block_rows, block_rows, KV_HEADS, group_size, HEAD)
    position_blocks = position.reshape(row_count // block_rows, block_rows)

    def attend(inputs):
        q_block, p_block = inputs
        scores = jnp.einsum('bcgd,kcd->cgbk', q_block.astype(jnp.float32), keys_wide) * HEAD ** (-0.5)
        visible = position[None, :] <= p_block[:, None]
        scores = jnp.where(visible, scores, -1e+30)
        row_peak = lax.optimization_barrier(jnp.max(scores, axis=-1, keepdims=True))
        weight = jnp.where(visible, jnp.exp(scores - row_peak), 0.0)
        row_total = lax.optimization_barrier(jnp.sum(weight, axis=-1))
        rounded = lax.optimization_barrier(weight.astype(jnp.bfloat16)).astype(jnp.float32)
        blended = jnp.einsum('cgbk,kcd->cgbd', rounded, values_wide) / row_total[..., None]
        return jnp.transpose(blended, (2, 0, 1, 3)).reshape(block_rows, HEADS * HEAD).astype(jnp.bfloat16)
    result = lax.map(attend, (query_blocks, position_blocks))
    return result.reshape(row_count, HEADS * HEAD)
```

```python
import functools
import math

import jax
import jax.numpy as jnp
import numpy as np
from jax import lax
from jax.experimental import pallas as pl
from jax.experimental.pallas import tpu as pltpu
from jax.sharding import PartitionSpec as P

HEADS = 16
KV_HEADS = 2
HEAD = 128
GROUP = HEADS // KV_HEADS
EPSILON = 1e-06
THETA = 1000000.0
SCALE = HEAD**-0.5 * math.log2(math.e)
HIDDEN = -1e30

VMEM = pltpu.VMEM
F32 = jnp.float32
BF16 = jnp.bfloat16


def partner(x, offset):
    return lax.ppermute(x, "ctx", [(i, i ^ offset) for i in range(lax.axis_size("ctx"))])


def tables(half, spans):
    inverse = THETA ** -(2.0 * np.arange(HEAD // 2) / HEAD)
    inverse = np.concatenate([inverse, inverse])[None, :]
    within = np.arange(half)[:, None] * inverse
    start = (np.arange(spans) * half)[:, None] * inverse
    return [jnp.asarray(f(a), F32) for a in (within, start) for f in (np.cos, np.sin)]


def rope(entries, cosine, sine):
    mean_square = jnp.mean(entries * entries, axis=-1, keepdims=True)
    turned = entries * cosine + pltpu.roll(entries, HEAD // 2, 1) * sine
    return turned * lax.rsqrt(mean_square + EPSILON)


def gained(gain_ref, cosine, sine):
    gain = gain_ref[...]
    lane = lax.broadcasted_iota(jnp.int32, sine.shape, 1)
    signed = jnp.where(lane < HEAD // 2, -sine, sine)
    return cosine * gain, signed * pltpu.roll(gain, HEAD // 2, 1)


def key_value_kernel(
    spans, hidden, norm_gain, w_key, w_value, key_gain, cos_in, sin_in, cos_at, sin_at, normed_out, kv_out, cos_out, sin_out
):
    own = lax.axis_index("ctx")
    half = cos_in.shape[0]
    for part in range(2):
        span = spans[own, part]
        cos_a, sin_a = cos_at[pl.ds(span, 1), :], sin_at[pl.ds(span, 1), :]
        cos_b, sin_b = cos_in[...], sin_in[...]
        rows = pl.ds(part * half, half)
        cos_out[rows, :] = cos_a * cos_b - sin_a * sin_b
        sin_out[rows, :] = sin_a * cos_b + cos_a * sin_b
    entries = hidden[...].astype(F32)
    mean_square = jnp.mean(entries * entries, axis=-1, keepdims=True)
    normed = (entries * lax.rsqrt(mean_square + EPSILON) * norm_gain[...]).astype(BF16)
    normed_out[...] = normed
    cosine, sine = gained(key_gain, cos_out[...], sin_out[...])
    keys = jnp.dot(normed, w_key[...], preferred_element_type=F32)
    for head in range(KV_HEADS):
        columns = slice(head * HEAD, (head + 1) * HEAD)
        kv_out[:, columns] = rope(keys[:, columns], cosine, sine).astype(BF16)
    values = jnp.dot(normed, w_value[...], preferred_element_type=F32)
    kv_out[:, KV_HEADS * HEAD :] = values.astype(BF16)


def query_kernel(normed, w_query, query_gain, cos, sin, out):
    cosine, sine = gained(query_gain, cos[...], sin[...])
    queries = jnp.dot(normed[...], w_query[...], preferred_element_type=F32)
    for head in range(out.shape[1] // HEAD):
        columns = slice(head * HEAD, (head + 1) * HEAD)
        out[:, columns] = rope(queries[:, columns], cosine, sine).astype(BF16)


def attention_kernel(devices, offsets, spans, queries, *refs):
    pieces = refs[: len(offsets)]
    out, kv, scores_a, scores_b, peak, total, accum, sem = refs[len(offsets) :]
    own = lax.axis_index("ctx")
    half = queries.shape[0] // 2
    lanes = GROUP * half
    unit = 4 * half
    span_0, span_1 = spans[own, 0], spans[own, 1]
    early_span = jnp.minimum(span_0, span_1)
    early_row = pl.multiple_of(jnp.where(span_0 < span_1, 0, half), half)
    rows_of = (pl.ds(early_row, half), pl.ds(pl.multiple_of(half - early_row, half), half))

    def fetch(piece, row, source):
        for part in range(2):
            pltpu.make_async_copy(
                piece.at[pl.ds(row + part * half, half), :],
                kv.at[pl.ds(pl.multiple_of(spans[source, part] * half, half), half), :],
                sem,
            ).start()

    for piece, sources in zip(pieces, offsets):
        if len(sources) == 1:
            fetch(piece, 0, own ^ sources[0])
        else:
            first = sources[0]

            @pl.loop(0, len(sources))
            def _(index, piece=piece, first=first):
                fetch(piece, pl.multiple_of(index * 2 * half, half), own ^ (first + index))

    pltpu.make_async_copy(kv, kv, sem).wait()

    a_units = devices // 4
    b_units = devices // 4 + 1
    early_units = early_span // 4 + 1

    def each(count, step):
        if count <= 8:
            for index in range(count):
                step(index)
        else:
            pl.loop(0, count)(step)

    def b_unit(index):
        late = jnp.where(index < early_units, 0, 1)
        first = jnp.where(index < early_units, index, index - early_units + a_units)
        return late, pl.multiple_of(first * unit, unit)

    def folded(x, reduce):
        return reduce(x.reshape(x.shape[0] // 8, 8, x.shape[1]), axis=0)

    for head in range(KV_HEADS):
        key_columns = pl.ds(head * HEAD, HEAD)
        value_columns = pl.ds((KV_HEADS + head) * HEAD, HEAD)

        def query_rows(rows):
            return jnp.concatenate(
                [queries[rows, (head * GROUP + g) * HEAD : (head * GROUP + g + 1) * HEAD] for g in range(GROUP)], axis=0
            )

        def score(key_rows, query):
            return lax.dot_general(
                kv[key_rows, key_columns], query, (((1,), (1,)), ((), ())), preferred_element_type=F32
            )

        late_query = query_rows(rows_of[1])
        peak[...] = jnp.full(peak.shape, HIDDEN, F32)
        total[...] = jnp.zeros(total.shape, F32)
        accum[...] = jnp.zeros(accum.shape, F32)

        def score_a(index):
            rows = pl.ds(index * unit, unit)
            scores = score(rows, late_query)
            scores_a[rows, :] = scores
            peak[1] = jnp.maximum(peak[1], folded(scores, jnp.max))

        def score_b(index):
            late, first = b_unit(index)
            query_row = pl.multiple_of(jnp.where(late == 1, half - early_row, early_row), half)
            scores = score(pl.ds(first, unit), query_rows(pl.ds(query_row, half)))
            span = jnp.where(late == 1, 2 * devices - 1 - early_span, early_span)
            key_at = first - span * half + lax.broadcasted_iota(jnp.int32, scores.shape, 0)
            query_at = lax.broadcasted_iota(jnp.int32, scores.shape, 1) % half
            scores = jnp.where(key_at <= query_at, scores, HIDDEN)
            scores_b[pl.ds(index * unit, unit), :] = scores
            peak[late] = jnp.maximum(peak[late], folded(scores, jnp.max))

        each(a_units, score_a)
        each(b_units, score_b)
        for late in range(2):
            peak[late] = jnp.broadcast_to(jnp.max(peak[late], axis=0, keepdims=True), (8, lanes))

        def add(scores, late, value_rows):
            weights = jnp.exp2((scores - peak[late][:1]) * SCALE)
            total[late] += folded(weights, jnp.sum)
            accum[late] += lax.dot_general(
                kv[value_rows, value_columns],
                weights.astype(BF16),
                (((0,), (0,)), ((), ())),
                preferred_element_type=F32,
            )

        def add_a(index):
            rows = pl.ds(index * unit, unit)
            add(scores_a[rows, :], 1, rows)

        def add_b(index):
            late, first = b_unit(index)
            add(scores_b[pl.ds(index * unit, unit), :], late, pl.ds(first, unit))

        each(a_units, add_a)
        each(b_units, add_b)
        for late in range(2):
            blended = accum[late] / jnp.sum(total[late], axis=0, keepdims=True)
            blended = blended.T.astype(BF16)
            for g in range(GROUP):
                column = (head * GROUP + g) * HEAD
                out[rows_of[late], column : column + HEAD] = blended[g * half : (g + 1) * half]


def body(hidden_in, span_order, norm_gain, w_query, w_key, w_value, query_gain, key_gain):
    rows, width = hidden_in.shape
    half = rows // 2
    devices = lax.axis_size("ctx")
    smem = pl.BlockSpec(memory_space=pltpu.SMEM)
    table = jax.ShapeDtypeStruct((rows, HEAD), F32)
    kv_width = 2 * KV_HEADS * HEAD

    normed, kv, cosine, sine = pl.pallas_call(
        key_value_kernel,
        out_shape=(
            jax.ShapeDtypeStruct((rows, width), BF16),
            jax.ShapeDtypeStruct((rows, kv_width), BF16),
            table,
            table,
        ),
        in_specs=[smem] + [pl.BlockSpec(memory_space=VMEM)] * 9,
        out_specs=[pl.BlockSpec(memory_space=VMEM)] * 4,
        name="key_value",
    )(
        span_order,
        hidden_in,
        norm_gain.reshape(1, width),
        w_key,
        w_value,
        key_gain.reshape(1, HEAD),
        *tables(half, 2 * devices),
    )

    tile = 512
    fixed = lambda shape: pl.BlockSpec(shape, lambda i: (0, 0))
    queries = pl.pallas_call(
        query_kernel,
        out_shape=jax.ShapeDtypeStruct((rows, HEADS * HEAD), BF16),
        grid=(HEADS * HEAD // tile,),
        in_specs=[
            fixed((rows, width)),
            pl.BlockSpec((width, tile), lambda i: (0, i)),
            fixed((1, HEAD)),
            fixed((rows, HEAD)),
            fixed((rows, HEAD)),
        ],
        out_specs=pl.BlockSpec((rows, tile), lambda i: (0, i)),
        cost_estimate=pl.CostEstimate(
            flops=2 * rows * width * HEADS * HEAD, bytes_accessed=2 * width * HEADS * HEAD, transcendentals=0
        ),
        name="query",
    )(normed, w_query, query_gain.reshape(1, HEAD), cosine, sine)

    pieces, offsets = [kv], [[0]]
    bits = [1 << b for b in range(devices.bit_length() - 1)]
    relayed = devices <= 16
    for bit in bits[:0:-1] + bits[:1] if relayed else bits:
        if not relayed:
            held = pieces[0] if len(pieces) == 1 else jnp.concatenate(pieces)
            flat = [o for group in offsets for o in group]
            pieces, offsets = [held], [flat]
        pieces, offsets = (
            pieces + [partner(piece, bit) for piece in pieces],
            offsets + [[o ^ bit for o in group] for group in offsets],
        )
    return attend(devices, offsets, span_order, queries, pieces)


def attend(devices, offsets, span_order, queries, pieces):
    rows = queries.shape[0]
    half = rows // 2
    lanes = GROUP * half
    kv_width = pieces[0].shape[1]
    a_rows = devices * half
    return pl.pallas_call(
        functools.partial(attention_kernel, devices, offsets),
        out_shape=jax.ShapeDtypeStruct((rows, HEADS * HEAD), BF16),
        in_specs=[pl.BlockSpec(memory_space=pltpu.SMEM), pl.BlockSpec(memory_space=VMEM)]
        + [pl.BlockSpec(memory_space=pltpu.HBM)] * len(pieces),
        out_specs=pl.BlockSpec(memory_space=VMEM),
        scratch_shapes=[
            VMEM((2 * a_rows, kv_width), BF16),
            VMEM((a_rows, lanes), F32),
            VMEM((a_rows + 4 * half, lanes), F32),
            VMEM((2, 8, lanes), F32),
            VMEM((2, 8, lanes), F32),
            VMEM((2, HEAD, lanes), F32),
            pltpu.SemaphoreType.DMA,
        ],
        compiler_params=pltpu.CompilerParams(vmem_limit_bytes=58 << 20),
        name="attention",
    )(span_order, queries, *pieces)


def solution(mesh):
    in_specs = (P(("groups", "ctx"), None), P("groups", None), P(), P(), P(), P(), P(), P())
    out_specs = P(("groups", "ctx"), None)
    return jax.shard_map(body, mesh=mesh, in_specs=in_specs, out_specs=out_specs, check_vma=False)
```

```python
import functools
import math

import jax
import jax.numpy as jnp
import numpy as np
from jax import lax
from jax.experimental import pallas as pl
from jax.experimental.pallas import tpu as pltpu
from jax.sharding import PartitionSpec as P


HEADS = 16
KV_HEADS = 2
HEAD = 128
GROUP = HEADS // KV_HEADS
EPSILON = 1e-06
THETA = 1000000.0
SCALE = HEAD**-0.5 * math.log2(math.e)
HIDDEN = -1e30
UNIT = 4
TILE = 512


VMEM = pltpu.VMEM
SMEM = pltpu.SMEM
F32 = jnp.float32
BF16 = jnp.bfloat16
DMA = pltpu.SemaphoreType.DMA


def placed(space):
    return pl.BlockSpec(memory_space=space)


def partner(x, offset):
    return lax.ppermute(x, "ctx", [(i, i ^ offset) for i in range(lax.axis_size("ctx"))])


def table(half, spans):
    inverse = THETA ** -(2.0 * np.arange(HEAD // 2) / HEAD)
    inverse = np.concatenate([inverse, inverse])[None, :]
    within = np.arange(half)[:, None] * inverse
    start = (np.arange(spans) * half)[:, None] * inverse
    return jnp.asarray(np.concatenate([np.cos(within), np.sin(within), np.cos(start), np.sin(start)]), F32)


def rope(entries, cosine, sine):
    square = entries * entries
    high = square.astype(BF16)
    low = (square - high.astype(F32)).astype(BF16)
    mean = jnp.full((HEAD, HEAD), 1.0 / HEAD, BF16)
    mean_square = jnp.dot(high, mean, preferred_element_type=F32) + jnp.dot(low, mean, preferred_element_type=F32)
    turned = entries * cosine + pltpu.roll(entries, HEAD // 2, 1) * sine
    return turned * lax.rsqrt(mean_square + EPSILON)


def gained(gain, angles):
    lane = lax.broadcasted_iota(jnp.int32, (angles.shape[0], HEAD), 1)
    cosine, sine = angles[:, :HEAD], angles[:, HEAD:]
    signed = jnp.where(lane < HEAD // 2, -sine, sine)
    return cosine * gain, signed * pltpu.roll(gain, HEAD // 2, 1)


def start_all(copies):
    copies = [pltpu.make_async_copy(*copy) for copy in copies]
    for copy in copies:
        copy.start()
    return copies


def key_value_kernel(
    spans_in, hidden_in, norm_gain_in, w_key_in, w_value_in, key_gain_in, query_gain_in, table_in, shared_out, kv_out,
    spans, hidden, norm_gain, w_key, w_value, key_gain, query_gain, steps, shared, angles, sems,
):
    width = hidden.shape[1]
    got_hidden, got_norm_gain, got_spans, got_steps, got_key_gain, got_query_gain, got_key, got_value = start_all(
        [
            (hidden_in, hidden, sems.at[0]),
            (norm_gain_in, norm_gain, sems.at[1]),
            (spans_in, spans, sems.at[2]),
            (table_in, steps, sems.at[3]),
            (key_gain_in, key_gain, sems.at[4]),
            (query_gain_in, query_gain, sems.at[5]),
            (w_key_in, w_key, sems.at[6]),
            (w_value_in, w_value, sems.at[7]),
        ]
    )
    own = lax.axis_index("ctx")
    half = hidden.shape[0] // 2
    count = (steps.shape[0] - 2 * half) // 2
    got_spans.wait()
    got_steps.wait()
    for part in range(2):
        span = spans[part, own]
        cos_a, sin_a = steps[pl.ds(2 * half + span, 1), :], steps[pl.ds(2 * half + count + span, 1), :]
        cos_b, sin_b = steps[:half], steps[half : 2 * half]
        rows = pl.ds(part * half, half)
        angles[rows, :HEAD] = cos_a * cos_b - sin_a * sin_b
        angles[rows, HEAD:] = sin_a * cos_b + cos_a * sin_b
    got_query_gain.wait()
    for part, turn in enumerate(gained(query_gain[...], angles[...])):
        for piece in range(3):
            column = width + (3 * part + piece) * HEAD
            rounded = turn.astype(BF16)
            shared[:, column : column + HEAD] = rounded
            turn = turn - rounded.astype(F32)
    got_hidden.wait()
    got_norm_gain.wait()
    entries = hidden[...].astype(F32)
    mean_square = jnp.mean(entries * entries, axis=-1, keepdims=True)
    shared[:, :width] = (entries * lax.rsqrt(mean_square + EPSILON) * norm_gain[...]).astype(BF16)
    put_shared = pltpu.make_async_copy(shared, shared_out, sems.at[0])
    put_shared.start()
    got_key_gain.wait()
    cosine, sine = gained(key_gain[...], angles[...])
    got_key.wait()
    keys = jnp.dot(shared[:, :width], w_key[...], preferred_element_type=F32)
    got_value.wait()
    for head in range(KV_HEADS):
        columns = slice(head * HEAD, (head + 1) * HEAD)
        kv_out[:, columns] = rope(keys[:, columns], cosine, sine).astype(BF16)
    values = jnp.dot(shared[:, :width], w_value[...], preferred_element_type=F32)
    kv_out[:, KV_HEADS * HEAD :] = values.astype(BF16)
    put_shared.wait()


def query_kernel(shared_in, w_query, out, shared, weights, product, sems):
    tiles, width, _ = weights.shape
    got_shared, *got = start_all(
        [(shared_in, shared, sems.at[0])]
        + [(w_query.at[:, pl.ds(i * TILE, TILE)], weights.at[i], sems.at[1 + i]) for i in range(tiles)]
    )
    got_shared.wait()
    pieces = [shared[:, width + i * HEAD : width + (i + 1) * HEAD].astype(F32) for i in range(6)]
    cosine, sine = (pieces[i] + pieces[i + 1] + pieces[i + 2] for i in (0, 3))
    for index in range(tiles + 1):
        if index < tiles:
            got[index].wait()
            product[index % 2] = jnp.dot(shared[:, :width], weights[index], preferred_element_type=F32)
        if index > 0:
            for head in range(TILE // HEAD):
                column = (index - 1) * TILE + head * HEAD
                entries = product[(index - 1) % 2][:, head * HEAD : (head + 1) * HEAD]
                out[:, column : column + HEAD] = rope(entries, cosine, sine).astype(BF16)


def unit_count(blocks, own):
    seen = blocks + 1 if own else blocks
    return max(-(-e // UNIT) - (-(seen - e) // UNIT) for e in range(1 if own else 0, blocks + 1))


def attention_kernel(devices, offsets, first, last, spans, queries, *refs):
    blocks = sum(len(group) for group in offsets)
    pieces, refs = refs[: len(offsets)], refs[len(offsets) :]
    if not first:
        (peak_in, total_in, accum_in), refs = refs[:3], refs[3:]
    if last:
        out, peak, total, accum, kv, scores_a, scores_b, packed, sem = refs
    else:
        peak, total, accum, kv, scores_a, scores_b, packed, sem = refs
    has_own = offsets[0][0] == 0
    own = lax.axis_index("ctx")
    half = queries.shape[0] // 2
    lanes = GROUP * half
    part_rows = kv.shape[0] // 2
    unit = UNIT * half

    def early_of(device):
        return jnp.minimum(spans[0, device], spans[1, device])

    def rows_in(device, base=0):
        row = jnp.where(spans[0, device] < spans[1, device], 0, half)
        return [pl.ds(pl.multiple_of(base + r, half), half) for r in (row, half - row)]

    mine = early_of(own)
    if blocks == devices:

        def fetch(piece, base, source):
            rank = early_of(source)
            for rows, at in zip(rows_in(source, base), (rank, 2 * blocks - 1 - rank)):
                to = pl.ds(pl.multiple_of(at * half, half), half)
                pltpu.make_async_copy(piece.at[rows, :], kv.at[to, :], sem).start()

        for piece, group in zip(pieces, offsets):

            @pl.loop(0, len(group))
            def _(index, piece=piece, group=group):
                fetch(piece, index * 2 * half, own ^ (group[0] + index))

        pltpu.make_async_copy(kv, kv, sem).wait()
        early_seen, late_seen = mine + 1, blocks - mine
    else:
        sources = [own ^ group[0] for group in offsets]
        early = [early_of(source) for source in sources]
        early_seen = sum((e <= mine).astype(jnp.int32) for e in early)
        late_seen = sum((e >= mine).astype(jnp.int32) for e in early)
        for part in range(2):
            if part_rows > blocks * half:
                pad = pl.ds(part * part_rows + blocks * half, part_rows - blocks * half)
                kv[pad, :] = jnp.zeros((part_rows - blocks * half, kv.shape[1]), BF16)
        for piece, source, e in zip(pieces, sources, early):
            rank = sum((other < e).astype(jnp.int32) for other in early)
            for rows, at in zip(rows_in(source), (rank * half, part_rows + (blocks - 1 - rank) * half)):
                kv[pl.ds(pl.multiple_of(at, half), half), :] = piece[rows, :]

    early_units = (early_seen + UNIT - 1) // UNIT
    a_steps = [(row, min(unit, blocks * half - row)) for row in range(0, blocks * half, unit)]
    b_units = unit_count(blocks, has_own)
    query_rows = rows_in(own)

    def each(count, step):
        if count <= 8:
            for index in range(count):
                step(index)
        else:
            pl.loop(0, count)(step)

    def a_rows(index):
        if len(a_steps) <= 8:
            return pl.ds(*a_steps[index])
        return pl.ds(pl.multiple_of(index * unit, unit), unit)

    def b_unit(index):
        late = jnp.where(index < early_units, 0, 1)
        start = jnp.where(index < early_units, index, index - early_units) * unit
        row = late * part_rows + jnp.minimum(start, part_rows - unit)
        seen = jnp.where(late == 1, late_seen, early_seen)
        return late, start - (seen - 1) * half, pl.ds(pl.multiple_of(row, half), unit)

    def b_rows(index):
        return pl.ds(index * unit if isinstance(index, int) else pl.multiple_of(index * unit, unit), unit)

    def slot(head):
        return head % scores_a.shape[0]

    def folded(x, reduce):
        return reduce(x.reshape(x.shape[0] // 8, 8, x.shape[1]), axis=0)

    def spread(x, reduce):
        return jnp.broadcast_to(reduce(x, axis=0, keepdims=True), (8, lanes))

    def score(head, rows, late):
        return lax.dot_general(
            kv[rows, pl.ds(head * HEAD, HEAD)], packed[head, late], (((1,), (1,)), ((), ())), preferred_element_type=F32
        )

    def find_scores(head):
        for late in range(2):
            for g in range(GROUP):
                column = (head * GROUP + g) * HEAD
                packed[head, late, g * half : (g + 1) * half, :] = queries[query_rows[late], column : column + HEAD]
            if first:
                peak[head, late] = jnp.full((8, lanes), HIDDEN, F32)
            else:
                peak[head, late] = peak_in[head, late]

        def step_a(index):
            scores = score(head, a_rows(index), 1)
            scores_a[slot(head), a_rows(index), :] = scores
            peak[head, 1] = jnp.maximum(peak[head, 1], folded(scores, jnp.max))

        def step_b(index):
            late, ahead, rows = b_unit(index)
            scores = score(head, rows, late)
            key_at = ahead + lax.broadcasted_iota(jnp.int32, scores.shape, 0)
            query_at = lax.broadcasted_iota(jnp.int32, scores.shape, 1) % half if has_own else half - 1
            scores = jnp.where(key_at <= query_at, scores, HIDDEN)
            scores_b[slot(head), b_rows(index), :] = scores
            peak[head, late] = jnp.maximum(peak[head, late], folded(scores, jnp.max))

        each(len(a_steps), step_a)
        each(b_units, step_b)

    def blend(head):
        for late in range(2):
            peak[head, late] = spread(peak[head, late], jnp.max)
            if first:
                total[head, late] = jnp.zeros((8, lanes), F32)
                accum[head, late] = jnp.zeros((HEAD, lanes), F32)
            else:
                decay = jnp.exp2((peak_in[head, late] - peak[head, late]) * SCALE)
                total[head, late] = total_in[head, late] * decay
                accum[head, late] = accum_in[head, late] * decay[:1]

        def add(scores, late, rows):
            weights = jnp.exp2((scores - peak[head, late][:1]) * SCALE)
            total[head, late] += folded(weights, jnp.sum)
            accum[head, late] += lax.dot_general(
                kv[rows, pl.ds((KV_HEADS + head) * HEAD, HEAD)],
                weights.astype(BF16),
                (((0,), (0,)), ((), ())),
                preferred_element_type=F32,
            )

        def step_a(index):
            add(scores_a[slot(head), a_rows(index), :], 1, a_rows(index))

        def step_b(index):
            late, _, rows = b_unit(index)
            add(scores_b[slot(head), b_rows(index), :], late, rows)

        each(len(a_steps), step_a)
        each(b_units, step_b)
        if last:
            for late in range(2):
                blended = accum[head, late] / jnp.sum(total[head, late], axis=0, keepdims=True)
                blended = blended.T.astype(BF16)
                for g in range(GROUP):
                    column = (head * GROUP + g) * HEAD
                    out[query_rows[late], column : column + HEAD] = blended[g * half : (g + 1) * half]

    for step in (find_scores, blend) if scores_a.shape[0] == KV_HEADS else (lambda head: (find_scores(head), blend(head)),):
        for head in range(KV_HEADS):
            step(head)


def attend(devices, offsets, spans, queries, pieces, state=(), last=True):
    rows = queries.shape[0]
    half = rows // 2
    lanes = GROUP * half
    blocks = sum(len(group) for group in offsets)
    part_rows = -(-blocks // UNIT) * UNIT * half
    b_rows = unit_count(blocks, offsets[0][0] == 0) * UNIT * half
    shapes = [(KV_HEADS, 2, 8, lanes), (KV_HEADS, 2, 8, lanes), (KV_HEADS, 2, HEAD, lanes)]
    states = [VMEM(shape, F32) for shape in shapes]
    relayed = len(offsets) == blocks
    slots = KV_HEADS if relayed else 1
    if last:
        out_shape, out_specs = jax.ShapeDtypeStruct((rows, HEADS * HEAD), BF16), placed(VMEM)
    else:
        out_shape, out_specs = [jax.ShapeDtypeStruct(shape, F32) for shape in shapes], [placed(VMEM)] * 3
    return pl.pallas_call(
        functools.partial(attention_kernel, devices, offsets, not state, last),
        out_shape=out_shape,
        in_specs=[placed(SMEM), placed(VMEM)]
        + [placed(VMEM if relayed else pl.ANY)] * len(pieces)
        + [placed(VMEM)] * len(state),
        out_specs=out_specs,
        scratch_shapes=(states if last else [])
        + [
            VMEM((2 * part_rows, pieces[0].shape[1]), BF16),
            VMEM((slots, blocks * half, lanes), F32),
            VMEM((slots, b_rows, lanes), F32),
            VMEM((KV_HEADS, 2, lanes, HEAD), BF16),
            DMA,
        ],
        compiler_params=pltpu.CompilerParams(vmem_limit_bytes=(20 if relayed else 63) << 20),
        cost_estimate=pl.CostEstimate(
            flops=8 * rows * rows * blocks * HEADS * HEAD // 2, bytes_accessed=2 * rows * HEADS * HEAD, transcendentals=0
        ),
        name="attention",
    )(spans, queries, *pieces, *state)


def body(hidden_in, span_order, norm_gain, w_query, w_key, w_value, query_gain, key_gain):
    rows, width = hidden_in.shape
    half = rows // 2
    devices = lax.axis_size("ctx")
    kv_width = 2 * KV_HEADS * HEAD
    steps = table(half, 2 * devices)
    span_order = span_order.T

    shared_width = width + 6 * HEAD
    shared, kv = pl.pallas_call(
        key_value_kernel,
        out_shape=(jax.ShapeDtypeStruct((rows, shared_width), BF16), jax.ShapeDtypeStruct((rows, kv_width), BF16)),
        in_specs=[placed(pl.ANY)] * 8,
        out_specs=[placed(pl.ANY), placed(VMEM)],
        scratch_shapes=[
            SMEM(span_order.shape, jnp.int32),
            VMEM((rows, width), BF16),
            VMEM((1, width), F32),
            VMEM(w_key.shape, BF16),
            VMEM(w_value.shape, BF16),
            VMEM((1, HEAD), F32),
            VMEM((1, HEAD), F32),
            VMEM(steps.shape, F32),
            VMEM((rows, shared_width), BF16),
            VMEM((rows, 2 * HEAD), F32),
            DMA((8,)),
        ],
        compiler_params=pltpu.CompilerParams(vmem_limit_bytes=63 << 20),
        name="key_value",
    )(
        span_order,
        hidden_in,
        norm_gain.reshape(1, width),
        w_key,
        w_value,
        key_gain.reshape(1, HEAD),
        query_gain.reshape(1, HEAD),
        steps,
    )

    tiles = HEADS * HEAD // TILE
    queries = pl.pallas_call(
        query_kernel,
        out_shape=jax.ShapeDtypeStruct((rows, HEADS * HEAD), BF16),
        in_specs=[placed(pl.ANY)] * 2,
        out_specs=placed(VMEM),
        scratch_shapes=[
            VMEM((rows, shared_width), BF16),
            VMEM((tiles, width, TILE), BF16),
            VMEM((2, rows, TILE), F32),
            DMA((1 + tiles,)),
        ],
        compiler_params=pltpu.CompilerParams(vmem_limit_bytes=53 << 20),
        cost_estimate=pl.CostEstimate(
            flops=2 * rows * width * HEADS * HEAD, bytes_accessed=2 * width * HEADS * HEAD, transcendentals=0
        ),
        name="query",
    )(shared, w_query)

    far = devices // 2
    if devices > 16:
        held, count = kv, 1
        while count < far:
            held = jnp.concatenate([held, partner(held, count)])
            count *= 2
        pieces, offsets = [held, partner(held, far)], [list(range(far)), list(range(far, devices))]
        return attend(devices, offsets, span_order, queries, pieces)

    def cores(pieces):
        for offset in list(pieces):
            pieces[offset + 1] = partner(pieces[offset], 1)
        return [[offset] for offset in pieces], list(pieces.values())

    near = range(2, far, 2)
    pieces = {0: kv, far: partner(kv, far)}
    for offset in near:
        pieces[offset] = partner(kv, offset)
    relayed = {}
    for offset in near:
        relayed[far + offset] = partner(pieces[far], offset)
    offsets, pieces = cores(pieces)
    state = attend(devices, offsets, span_order, queries, pieces, last=False)
    offsets, pieces = cores(relayed)
    return attend(devices, offsets, span_order, queries, pieces, state)


def solution(mesh):
    in_specs = (P(("groups", "ctx"), None), P("groups", None), P(), P(), P(), P(), P(), P())
    out_specs = P(("groups", "ctx"), None)
    return jax.shard_map(body, mesh=mesh, in_specs=in_specs, out_specs=out_specs, check_vma=False)
```

```python
import functools
import math

import jax
import jax.numpy as jnp
import numpy as np
from jax import lax
from jax.experimental import pallas as pl
from jax.experimental.pallas import tpu as pltpu
from jax.sharding import PartitionSpec as P


HEADS = 16
KV_HEADS = 2
HEAD = 128
GROUP = HEADS // KV_HEADS
EPSILON = 1e-06
THETA = 1000000.0
SCALE = HEAD**-0.5 * math.log2(math.e)
HIDDEN = -1e30
UNIT = 2
TILE = 512


VMEM = pltpu.VMEM
SMEM = pltpu.SMEM
F32 = jnp.float32
BF16 = jnp.bfloat16
DMA = pltpu.SemaphoreType.DMA


def placed(space):
    return pl.BlockSpec(memory_space=space)


def partner(x, offset):
    return lax.ppermute(x, "ctx", [(i, i ^ offset) for i in range(lax.axis_size("ctx"))])


def table(half, spans):
    inverse = THETA ** -(2.0 * np.arange(HEAD // 2) / HEAD)
    inverse = np.concatenate([inverse, inverse])[None, :]
    within = np.arange(half)[:, None] * inverse
    start = (np.arange(spans) * half)[:, None] * inverse
    return jnp.asarray(np.concatenate([np.cos(within), np.sin(within), np.cos(start), np.sin(start)]), F32)


def rope(entries, cosine, sine):
    square = entries * entries
    high = square.astype(BF16)
    low = (square - high.astype(F32)).astype(BF16)
    mean = jnp.full((HEAD, HEAD), 1.0 / HEAD, BF16)
    mean_square = jnp.dot(high, mean, preferred_element_type=F32) + jnp.dot(low, mean, preferred_element_type=F32)
    turned = entries * cosine + pltpu.roll(entries, HEAD // 2, 1) * sine
    return turned * lax.rsqrt(mean_square + EPSILON)


def gained(gain, angles):
    lane = lax.broadcasted_iota(jnp.int32, (angles.shape[0], HEAD), 1)
    cosine, sine = angles[:, :HEAD], angles[:, HEAD:]
    signed = jnp.where(lane < HEAD // 2, -sine, sine)
    return cosine * gain, signed * pltpu.roll(gain, HEAD // 2, 1)


def start_all(copies):
    copies = [pltpu.make_async_copy(*copy) for copy in copies]
    for copy in copies:
        copy.start()
    return copies


def key_value_kernel(
    spans_in, hidden_in, norm_gain_in, w_key_in, w_value_in, key_gain_in, query_gain_in, table_in, shared_out, kv_out,
    spans, hidden, norm_gain, w_key, w_value, key_gain, query_gain, steps, shared, angles, sems,
):
    width = hidden.shape[1]
    got_hidden, got_norm_gain, got_spans, got_steps, got_key_gain, got_query_gain, got_key, got_value = start_all(
        [
            (hidden_in, hidden, sems.at[0]),
            (norm_gain_in, norm_gain, sems.at[1]),
            (spans_in, spans, sems.at[2]),
            (table_in, steps, sems.at[3]),
            (key_gain_in, key_gain, sems.at[4]),
            (query_gain_in, query_gain, sems.at[5]),
            (w_key_in, w_key, sems.at[6]),
            (w_value_in, w_value, sems.at[7]),
        ]
    )
    own = lax.axis_index("ctx")
    half = hidden.shape[0] // 2
    count = (steps.shape[0] - 2 * half) // 2
    got_spans.wait()
    got_steps.wait()
    for part in range(2):
        span = spans[part, own]
        cos_a, sin_a = steps[pl.ds(2 * half + span, 1), :], steps[pl.ds(2 * half + count + span, 1), :]
        cos_b, sin_b = steps[:half], steps[half : 2 * half]
        rows = pl.ds(part * half, half)
        angles[rows, :HEAD] = cos_a * cos_b - sin_a * sin_b
        angles[rows, HEAD:] = sin_a * cos_b + cos_a * sin_b
    got_query_gain.wait()
    for part, turn in enumerate(gained(query_gain[...], angles[...])):
        for piece in range(3):
            column = width + (3 * part + piece) * HEAD
            rounded = turn.astype(BF16)
            shared[:, column : column + HEAD] = rounded
            turn = turn - rounded.astype(F32)
    got_hidden.wait()
    got_norm_gain.wait()
    entries = hidden[...].astype(F32)
    mean_square = jnp.mean(entries * entries, axis=-1, keepdims=True)
    shared[:, :width] = (entries * lax.rsqrt(mean_square + EPSILON) * norm_gain[...]).astype(BF16)
    put_shared = pltpu.make_async_copy(shared, shared_out, sems.at[0])
    put_shared.start()
    got_key_gain.wait()
    cosine, sine = gained(key_gain[...], angles[...])
    got_key.wait()
    keys = jnp.dot(shared[:, :width], w_key[...], preferred_element_type=F32)
    got_value.wait()
    for head in range(KV_HEADS):
        columns = slice(head * HEAD, (head + 1) * HEAD)
        kv_out[:, columns] = rope(keys[:, columns], cosine, sine).astype(BF16)
    values = jnp.dot(shared[:, :width], w_value[...], preferred_element_type=F32)
    kv_out[:, KV_HEADS * HEAD :] = values.astype(BF16)
    put_shared.wait()


def query_kernel(shared_in, w_query, out, shared, weights, product, sems):
    tiles, width, _ = weights.shape
    got_shared, *got = start_all(
        [(shared_in, shared, sems.at[0])]
        + [(w_query.at[:, pl.ds(i * TILE, TILE)], weights.at[i], sems.at[1 + i]) for i in range(tiles)]
    )
    got_shared.wait()
    pieces = [shared[:, width + i * HEAD : width + (i + 1) * HEAD].astype(F32) for i in range(6)]
    cosine, sine = (pieces[i] + pieces[i + 1] + pieces[i + 2] for i in (0, 3))
    for index in range(tiles + 1):
        if index < tiles:
            got[index].wait()
            product[index % 2] = jnp.dot(shared[:, :width], weights[index], preferred_element_type=F32)
        if index > 0:
            for head in range(TILE // HEAD):
                column = (index - 1) * TILE + head * HEAD
                entries = product[(index - 1) % 2][:, head * HEAD : (head + 1) * HEAD]
                out[:, column : column + HEAD] = rope(entries, cosine, sine).astype(BF16)


def unit_count(blocks, own):
    seen = blocks + 1 if own else blocks
    return max(-(-e // UNIT) - (-(seen - e) // UNIT) for e in range(1 if own else 0, blocks + 1))


def attention_kernel(devices, offsets, first, last, spans, queries, *refs):
    blocks = sum(len(group) for group in offsets)
    pieces, refs = refs[: len(offsets)], refs[len(offsets) :]
    if not first:
        (peak_in, total_in, accum_in), refs = refs[:3], refs[3:]
    if last:
        out, peak, total, accum, kv, scores_a, scores_b, packed, sem = refs
    else:
        peak, total, accum, kv, scores_a, scores_b, packed, sem = refs
    has_own = offsets[0][0] == 0
    own = lax.axis_index("ctx")
    half = queries.shape[0] // 2
    lanes = GROUP * half
    part_rows = kv.shape[0] // 2
    unit = UNIT * half

    def early_of(device):
        return jnp.minimum(spans[0, device], spans[1, device])

    def rows_in(device, base=0):
        row = jnp.where(spans[0, device] < spans[1, device], 0, half)
        return [pl.ds(pl.multiple_of(base + r, half), half) for r in (row, half - row)]

    mine = early_of(own)
    if blocks == devices:

        def fetch(piece, base, source):
            rank = early_of(source)
            for rows, at in zip(rows_in(source, base), (rank, 2 * blocks - 1 - rank)):
                to = pl.ds(pl.multiple_of(at * half, half), half)
                pltpu.make_async_copy(piece.at[rows, :], kv.at[to, :], sem).start()

        for piece, group in zip(pieces, offsets):

            @pl.loop(0, len(group))
            def _(index, piece=piece, group=group):
                fetch(piece, index * 2 * half, own ^ (group[0] + index))

        pltpu.make_async_copy(kv, kv, sem).wait()
        early_seen, late_seen = mine + 1, blocks - mine
    else:
        sources = [own ^ group[0] for group in offsets]
        early = [early_of(source) for source in sources]
        early_seen = sum((e <= mine).astype(jnp.int32) for e in early)
        late_seen = sum((e >= mine).astype(jnp.int32) for e in early)
        for part in range(2):
            if part_rows > blocks * half:
                pad = pl.ds(part * part_rows + blocks * half, part_rows - blocks * half)
                kv[pad, :] = jnp.zeros((part_rows - blocks * half, kv.shape[1]), BF16)
        for piece, source, e in zip(pieces, sources, early):
            rank = sum((other < e).astype(jnp.int32) for other in early)
            for rows, at in zip(rows_in(source), (rank * half, part_rows + (blocks - 1 - rank) * half)):
                kv[pl.ds(pl.multiple_of(at, half), half), :] = piece[rows, :]

    early_units = (early_seen + UNIT - 1) // UNIT
    a_steps = [(row, min(unit, blocks * half - row)) for row in range(0, blocks * half, unit)]
    b_units = unit_count(blocks, has_own)
    query_rows = rows_in(own)

    def each(count, step):
        if count <= 8:
            for index in range(count):
                step(index)
        else:
            pl.loop(0, count)(step)

    def a_rows(index):
        if len(a_steps) <= 8:
            return pl.ds(*a_steps[index])
        return pl.ds(pl.multiple_of(index * unit, unit), unit)

    def b_unit(index):
        late = jnp.where(index < early_units, 0, 1)
        start = jnp.where(index < early_units, index, index - early_units) * unit
        row = late * part_rows + jnp.minimum(start, part_rows - unit)
        seen = jnp.where(late == 1, late_seen, early_seen)
        return late, start - (seen - 1) * half, pl.ds(pl.multiple_of(row, half), unit)

    def b_rows(index):
        return pl.ds(index * unit if isinstance(index, int) else pl.multiple_of(index * unit, unit), unit)

    def slot(head):
        return head % scores_a.shape[0]

    def folded(x, reduce):
        return reduce(x.reshape(x.shape[0] // 8, 8, x.shape[1]), axis=0)

    def spread(x, reduce):
        return jnp.broadcast_to(reduce(x, axis=0, keepdims=True), (8, lanes))

    def score(head, rows, late):
        return lax.dot_general(
            kv[rows, pl.ds(head * HEAD, HEAD)], packed[head, late], (((1,), (1,)), ((), ())), preferred_element_type=F32
        )

    def find_scores(head):
        for late in range(2):
            for g in range(GROUP):
                column = (head * GROUP + g) * HEAD
                packed[head, late, g * half : (g + 1) * half, :] = queries[query_rows[late], column : column + HEAD]
            if first:
                peak[head, late] = jnp.full((8, lanes), HIDDEN, F32)
            else:
                peak[head, late] = peak_in[head, late]

        def step_a(index):
            scores = score(head, a_rows(index), 1)
            scores_a[slot(head), a_rows(index), :] = scores
            peak[head, 1] = jnp.maximum(peak[head, 1], folded(scores, jnp.max))

        def step_b(index):
            late, ahead, rows = b_unit(index)
            scores = score(head, rows, late)
            key_at = ahead + lax.broadcasted_iota(jnp.int32, scores.shape, 0)
            query_at = lax.broadcasted_iota(jnp.int32, scores.shape, 1) % half if has_own else half - 1
            scores = jnp.where(key_at <= query_at, scores, HIDDEN)
            scores_b[slot(head), b_rows(index), :] = scores
            peak[head, late] = jnp.maximum(peak[head, late], folded(scores, jnp.max))

        each(len(a_steps), step_a)
        each(b_units, step_b)

    def blend(head):
        for late in range(2):
            peak[head, late] = spread(peak[head, late], jnp.max)
            if first:
                total[head, late] = jnp.zeros((8, lanes), F32)
                accum[head, late] = jnp.zeros((HEAD, lanes), F32)
            else:
                decay = jnp.exp2((peak_in[head, late] - peak[head, late]) * SCALE)
                total[head, late] = total_in[head, late] * decay
                accum[head, late] = accum_in[head, late] * decay[:1]

        def add(scores, late, rows):
            weights = jnp.exp2((scores - peak[head, late][:1]) * SCALE)
            total[head, late] += folded(weights, jnp.sum)
            accum[head, late] += lax.dot_general(
                kv[rows, pl.ds((KV_HEADS + head) * HEAD, HEAD)],
                weights.astype(BF16),
                (((0,), (0,)), ((), ())),
                preferred_element_type=F32,
            )

        def step_a(index):
            add(scores_a[slot(head), a_rows(index), :], 1, a_rows(index))

        def step_b(index):
            late, _, rows = b_unit(index)
            add(scores_b[slot(head), b_rows(index), :], late, rows)

        each(len(a_steps), step_a)
        each(b_units, step_b)
        if last:
            for late in range(2):
                blended = accum[head, late] * (1.0 / jnp.sum(total[head, late], axis=0, keepdims=True))
                blended = blended.astype(BF16).T
                for g in range(GROUP):
                    column = (head * GROUP + g) * HEAD
                    out[query_rows[late], column : column + HEAD] = blended[g * half : (g + 1) * half]

    for step in (find_scores, blend) if scores_a.shape[0] == KV_HEADS else (lambda head: (find_scores(head), blend(head)),):
        for head in range(KV_HEADS):
            step(head)


def attend(devices, offsets, spans, queries, pieces, state=(), last=True):
    rows = queries.shape[0]
    half = rows // 2
    lanes = GROUP * half
    blocks = sum(len(group) for group in offsets)
    part_rows = -(-blocks // UNIT) * UNIT * half
    b_rows = unit_count(blocks, offsets[0][0] == 0) * UNIT * half
    shapes = [(KV_HEADS, 2, 8, lanes), (KV_HEADS, 2, 8, lanes), (KV_HEADS, 2, HEAD, lanes)]
    states = [VMEM(shape, F32) for shape in shapes]
    relayed = len(offsets) == blocks
    slots = KV_HEADS if relayed else 1
    if last:
        out_shape, out_specs = jax.ShapeDtypeStruct((rows, HEADS * HEAD), BF16), placed(VMEM)
    else:
        out_shape, out_specs = [jax.ShapeDtypeStruct(shape, F32) for shape in shapes], [placed(VMEM)] * 3
    return pl.pallas_call(
        functools.partial(attention_kernel, devices, offsets, not state, last),
        out_shape=out_shape,
        in_specs=[placed(SMEM), placed(VMEM)]
        + [placed(VMEM if relayed else pl.ANY)] * len(pieces)
        + [placed(VMEM)] * len(state),
        out_specs=out_specs,
        scratch_shapes=(states if last else [])
        + [
            VMEM((2 * part_rows, pieces[0].shape[1]), BF16),
            VMEM((slots, blocks * half, lanes), F32),
            VMEM((slots, b_rows, lanes), F32),
            VMEM((KV_HEADS, 2, lanes, HEAD), BF16),
            DMA,
        ],
        compiler_params=pltpu.CompilerParams(vmem_limit_bytes=(20 if relayed else 63) << 20),
        cost_estimate=pl.CostEstimate(
            flops=8 * rows * rows * blocks * HEADS * HEAD // 2, bytes_accessed=2 * rows * HEADS * HEAD, transcendentals=0
        ),
        name="attention",
    )(spans, queries, *pieces, *state)


def body(hidden_in, span_order, norm_gain, w_query, w_key, w_value, query_gain, key_gain):
    rows, width = hidden_in.shape
    half = rows // 2
    devices = lax.axis_size("ctx")
    kv_width = 2 * KV_HEADS * HEAD
    steps = table(half, 2 * devices)
    span_order = span_order.T

    shared_width = width + 6 * HEAD
    shared, kv = pl.pallas_call(
        key_value_kernel,
        out_shape=(jax.ShapeDtypeStruct((rows, shared_width), BF16), jax.ShapeDtypeStruct((rows, kv_width), BF16)),
        in_specs=[placed(pl.ANY)] * 8,
        out_specs=[placed(pl.ANY), placed(VMEM)],
        scratch_shapes=[
            SMEM(span_order.shape, jnp.int32),
            VMEM((rows, width), BF16),
            VMEM((1, width), F32),
            VMEM(w_key.shape, BF16),
            VMEM(w_value.shape, BF16),
            VMEM((1, HEAD), F32),
            VMEM((1, HEAD), F32),
            VMEM(steps.shape, F32),
            VMEM((rows, shared_width), BF16),
            VMEM((rows, 2 * HEAD), F32),
            DMA((8,)),
        ],
        compiler_params=pltpu.CompilerParams(vmem_limit_bytes=63 << 20),
        name="key_value",
    )(
        span_order,
        hidden_in,
        norm_gain.reshape(1, width),
        w_key,
        w_value,
        key_gain.reshape(1, HEAD),
        query_gain.reshape(1, HEAD),
        steps,
    )

    tiles = HEADS * HEAD // TILE
    queries = pl.pallas_call(
        query_kernel,
        out_shape=jax.ShapeDtypeStruct((rows, HEADS * HEAD), BF16),
        in_specs=[placed(pl.ANY)] * 2,
        out_specs=placed(VMEM),
        scratch_shapes=[
            VMEM((rows, shared_width), BF16),
            VMEM((tiles, width, TILE), BF16),
            VMEM((2, rows, TILE), F32),
            DMA((1 + tiles,)),
        ],
        compiler_params=pltpu.CompilerParams(vmem_limit_bytes=53 << 20),
        cost_estimate=pl.CostEstimate(
            flops=2 * rows * width * HEADS * HEAD, bytes_accessed=2 * width * HEADS * HEAD, transcendentals=0
        ),
        name="query",
    )(shared, w_query)

    far = devices // 2
    if devices > 16:
        held, count = kv, 1
        while count < far:
            held = jnp.concatenate([held, partner(held, count)])
            count *= 2
        pieces, offsets = [held, partner(held, far)], [list(range(far)), list(range(far, devices))]
        return attend(devices, offsets, span_order, queries, pieces)

    def cores(pieces):
        for offset in list(pieces):
            pieces[offset + 1] = partner(pieces[offset], 1)
        return [[offset] for offset in pieces], list(pieces.values())

    near = range(2, far, 2)
    pieces = {0: kv, far: partner(kv, far)}
    for offset in near:
        pieces[offset] = partner(kv, offset)
    relayed = {}
    for offset in near:
        relayed[far + offset] = partner(pieces[far], offset)
    offsets, pieces = cores(pieces)
    state = attend(devices, offsets, span_order, queries, pieces, last=False)
    offsets, pieces = cores(relayed)
    return attend(devices, offsets, span_order, queries, pieces, state)


def solution(mesh):
    in_specs = (P(("groups", "ctx"), None), P("groups", None), P(), P(), P(), P(), P(), P())
    out_specs = P(("groups", "ctx"), None)
    return jax.shard_map(body, mesh=mesh, in_specs=in_specs, out_specs=out_specs, check_vma=False)
```

```python
import functools
import math

import jax
import jax.numpy as jnp
import numpy as np
from jax import lax
from jax.experimental import pallas as pl
from jax.experimental.pallas import tpu as pltpu
from jax.sharding import PartitionSpec as P


HEADS = 16
KV_HEADS = 2
HEAD = 128
GROUP = HEADS // KV_HEADS
EPSILON = 1e-06
THETA = 1000000.0
SCALE = HEAD**-0.5 * math.log2(math.e)
HIDDEN = -1e30
UNIT = 2
TILE = 512


VMEM = pltpu.VMEM
SMEM = pltpu.SMEM
F32 = jnp.float32
BF16 = jnp.bfloat16
DMA = pltpu.SemaphoreType.DMA


def placed(space):
    return pl.BlockSpec(memory_space=space)


def partner(x, offset):
    return lax.ppermute(x, "ctx", [(i, i ^ offset) for i in range(lax.axis_size("ctx"))])


def table(half, spans):
    inverse = THETA ** -(2.0 * np.arange(HEAD // 2) / HEAD)
    inverse = np.concatenate([inverse, inverse])[None, :]
    within = np.arange(half)[:, None] * inverse
    start = (np.arange(spans) * half)[:, None] * inverse
    return jnp.asarray(np.concatenate([np.cos(within), np.sin(within), np.cos(start), np.sin(start)]), F32)


def rope(entries, cosine, sine):
    square = entries * entries
    high = square.astype(BF16)
    low = (square - high.astype(F32)).astype(BF16)
    mean = jnp.full((HEAD, HEAD), 1.0 / HEAD, BF16)
    mean_square = jnp.dot(high, mean, preferred_element_type=F32) + jnp.dot(low, mean, preferred_element_type=F32)
    turned = entries * cosine + pltpu.roll(entries, HEAD // 2, 1) * sine
    return turned * lax.rsqrt(mean_square + EPSILON)


def gained(gain, angles):
    lane = lax.broadcasted_iota(jnp.int32, (angles.shape[0], HEAD), 1)
    cosine, sine = angles[:, :HEAD], angles[:, HEAD:]
    signed = jnp.where(lane < HEAD // 2, -sine, sine)
    return cosine * gain, signed * pltpu.roll(gain, HEAD // 2, 1)


def start_all(copies):
    copies = [pltpu.make_async_copy(*copy) for copy in copies]
    for copy in copies:
        copy.start()
    return copies


def key_value_kernel(
    spans_in, hidden_in, norm_gain_in, w_key_in, w_value_in, key_gain_in, query_gain_in, table_in, shared_out, kv_out,
    spans, hidden, norm_gain, w_key, w_value, key_gain, query_gain, steps, shared, angles, sems,
):
    width = hidden.shape[1]
    got_hidden, got_norm_gain, got_spans, got_steps, got_key_gain, got_query_gain, got_key, got_value = start_all(
        [
            (hidden_in, hidden, sems.at[0]),
            (norm_gain_in, norm_gain, sems.at[1]),
            (spans_in, spans, sems.at[2]),
            (table_in, steps, sems.at[3]),
            (key_gain_in, key_gain, sems.at[4]),
            (query_gain_in, query_gain, sems.at[5]),
            (w_key_in, w_key, sems.at[6]),
            (w_value_in, w_value, sems.at[7]),
        ]
    )
    own = lax.axis_index("ctx")
    half = hidden.shape[0] // 2
    count = (steps.shape[0] - 2 * half) // 2
    got_spans.wait()
    got_steps.wait()
    for part in range(2):
        span = spans[part, own]
        cos_a, sin_a = steps[pl.ds(2 * half + span, 1), :], steps[pl.ds(2 * half + count + span, 1), :]
        cos_b, sin_b = steps[:half], steps[half : 2 * half]
        rows = pl.ds(part * half, half)
        angles[rows, :HEAD] = cos_a * cos_b - sin_a * sin_b
        angles[rows, HEAD:] = sin_a * cos_b + cos_a * sin_b
    got_query_gain.wait()
    for part, turn in enumerate(gained(query_gain[...], angles[...])):
        for piece in range(3):
            column = width + (3 * part + piece) * HEAD
            rounded = turn.astype(BF16)
            shared[:, column : column + HEAD] = rounded
            turn = turn - rounded.astype(F32)
    got_hidden.wait()
    got_norm_gain.wait()
    entries = hidden[...].astype(F32)
    mean_square = jnp.mean(entries * entries, axis=-1, keepdims=True)
    shared[:, :width] = (entries * lax.rsqrt(mean_square + EPSILON) * norm_gain[...]).astype(BF16)
    put_shared = pltpu.make_async_copy(shared, shared_out, sems.at[0])
    put_shared.start()
    got_key_gain.wait()
    cosine, sine = gained(key_gain[...], angles[...])
    got_key.wait()
    keys = jnp.dot(shared[:, :width], w_key[...], preferred_element_type=F32)
    got_value.wait()
    for head in range(KV_HEADS):
        columns = slice(head * HEAD, (head + 1) * HEAD)
        kv_out[:, columns] = rope(keys[:, columns], cosine, sine).astype(BF16)
    values = jnp.dot(shared[:, :width], w_value[...], preferred_element_type=F32)
    kv_out[:, KV_HEADS * HEAD :] = values.astype(BF16)
    put_shared.wait()


def query_kernel(shared_in, w_query, out, shared, weights, product, sems):
    tiles, width, _ = weights.shape
    got_shared, *got = start_all(
        [(shared_in, shared, sems.at[0])]
        + [(w_query.at[:, pl.ds(i * TILE, TILE)], weights.at[i], sems.at[1 + i]) for i in range(tiles)]
    )
    got_shared.wait()
    pieces = [shared[:, width + i * HEAD : width + (i + 1) * HEAD].astype(F32) for i in range(6)]
    cosine, sine = (pieces[i] + pieces[i + 1] + pieces[i + 2] for i in (0, 3))
    for index in range(tiles + 1):
        if index < tiles:
            got[index].wait()
            product[index % 2] = jnp.dot(shared[:, :width], weights[index], preferred_element_type=F32)
        if index > 0:
            for head in range(TILE // HEAD):
                column = (index - 1) * TILE + head * HEAD
                entries = product[(index - 1) % 2][:, head * HEAD : (head + 1) * HEAD]
                out[:, column : column + HEAD] = rope(entries, cosine, sine).astype(BF16)


def unit_count(blocks, own):
    seen = blocks + 1 if own else blocks
    return max(-(-e // UNIT) - (-(seen - e) // UNIT) for e in range(1 if own else 0, blocks + 1))


def attention_kernel(devices, offsets, first, last, spans, queries, *refs):
    blocks = sum(len(group) for group in offsets)
    pieces, refs = refs[: len(offsets)], refs[len(offsets) :]
    heads = KV_HEADS

    def per_head(refs):
        return [refs[i * heads : (i + 1) * heads] for i in range(3)]

    if not first:
        (peak_in, total_in, accum_in), refs = per_head(refs), refs[3 * heads :]
    if last:
        out, refs = refs[0], refs[1:]
    (peak, total, accum), refs = per_head(refs), refs[3 * heads :]
    kv, scores_a, scores_b, packed, result, sem, put_sems = refs
    has_own = offsets[0][0] == 0
    own = lax.axis_index("ctx")
    half = queries.shape[0] // 2
    lanes = GROUP * half
    part_rows = kv.shape[0] // 2
    unit = UNIT * half

    def early_of(device):
        return jnp.minimum(spans[0, device], spans[1, device])

    def rows_in(device, base=0):
        row = jnp.where(spans[0, device] < spans[1, device], 0, half)
        return [pl.ds(pl.multiple_of(base + r, half), half) for r in (row, half - row)]

    mine = early_of(own)
    if blocks == devices:

        def fetch(piece, base, source):
            rank = early_of(source)
            for rows, at in zip(rows_in(source, base), (rank, 2 * blocks - 1 - rank)):
                to = pl.ds(pl.multiple_of(at * half, half), half)
                pltpu.make_async_copy(piece.at[rows, :], kv.at[to, :], sem).start()

        for piece, group in zip(pieces, offsets):

            @pl.loop(0, len(group))
            def _(index, piece=piece, group=group):
                fetch(piece, index * 2 * half, own ^ (group[0] + index))

        pltpu.make_async_copy(kv, kv, sem).wait()
        early_seen, late_seen = mine + 1, blocks - mine
    else:
        sources = [own ^ group[0] for group in offsets]
        early = [early_of(source) for source in sources]
        early_seen = sum((e <= mine).astype(jnp.int32) for e in early)
        late_seen = sum((e >= mine).astype(jnp.int32) for e in early)
        for part in range(2):
            if part_rows > blocks * half:
                pad = pl.ds(part * part_rows + blocks * half, part_rows - blocks * half)
                kv[pad, :] = jnp.zeros((part_rows - blocks * half, kv.shape[1]), BF16)
        for piece, source, e in zip(pieces, sources, early):
            rank = sum((other < e).astype(jnp.int32) for other in early)
            for rows, at in zip(rows_in(source), (rank * half, part_rows + (blocks - 1 - rank) * half)):
                kv[pl.ds(pl.multiple_of(at, half), half), :] = piece[rows, :]

    early_units = (early_seen + UNIT - 1) // UNIT
    a_steps = [(row, min(unit, blocks * half - row)) for row in range(0, blocks * half, unit)]
    b_units = unit_count(blocks, has_own)
    query_rows = rows_in(own)

    def each(count, step):
        if count <= 8:
            for index in range(count):
                step(index)
                yield
        else:
            pl.loop(0, count)(step)

    def a_rows(index):
        if len(a_steps) <= 8:
            return pl.ds(*a_steps[index])
        return pl.ds(pl.multiple_of(index * unit, unit), unit)

    def b_unit(index):
        late = jnp.where(index < early_units, 0, 1)
        start = jnp.where(index < early_units, index, index - early_units) * unit
        row = late * part_rows + jnp.minimum(start, part_rows - unit)
        seen = jnp.where(late == 1, late_seen, early_seen)
        return late, start - (seen - 1) * half, pl.ds(pl.multiple_of(row, half), unit)

    def b_rows(index):
        return pl.ds(index * unit if isinstance(index, int) else pl.multiple_of(index * unit, unit), unit)

    def slot(head):
        return head % scores_a.shape[0]

    def folded(x, reduce):
        return reduce(x.reshape(x.shape[0] // 8, 8, x.shape[1]), axis=0)

    def spread(x, reduce):
        return jnp.broadcast_to(reduce(x, axis=0, keepdims=True), (8, lanes))

    def score(head, rows, late):
        return lax.dot_general(
            kv[rows, pl.ds(head * HEAD, HEAD)], packed[head, late], (((1,), (1,)), ((), ())), preferred_element_type=F32
        )

    def find_scores(head):
        for late in range(2):
            for g in range(GROUP):
                column = (head * GROUP + g) * HEAD
                packed[head, late, g * half : (g + 1) * half, :] = queries[query_rows[late], column : column + HEAD]
            if first:
                peak[head][late] = jnp.full((8, lanes), HIDDEN, F32)
            else:
                peak[head][late] = peak_in[head][late]

        def step_a(index):
            scores = score(head, a_rows(index), 1)
            scores_a[slot(head), a_rows(index), :] = scores
            peak[head][1] = jnp.maximum(peak[head][1], folded(scores, jnp.max))

        def step_b(index):
            late, ahead, rows = b_unit(index)
            scores = score(head, rows, late)
            key_at = ahead + lax.broadcasted_iota(jnp.int32, (unit, HEAD), 0)
            query_at = lax.broadcasted_iota(jnp.int32, (unit, HEAD), 1) % half if has_own else half - 1
            limit = jnp.where(key_at <= query_at, -HIDDEN, HIDDEN)
            scores = jnp.minimum(scores, jnp.concatenate([limit] * (lanes // HEAD), axis=1))
            scores_b[slot(head), b_rows(index), :] = scores
            peak[head][late] = jnp.maximum(peak[head][late], folded(scores, jnp.max))

        yield from each(len(a_steps), step_a)
        yield from each(b_units, step_b)

    def blend(head):
        for late in range(2):
            peak[head][late] = spread(peak[head][late], jnp.max)
            if first:
                total[head][late] = jnp.zeros((8, lanes), F32)
                accum[head][late] = jnp.zeros((HEAD, lanes), F32)
            else:
                decay = jnp.exp2((peak_in[head][late] - peak[head][late]) * SCALE)
                total[head][late] = total_in[head][late] * decay
                accum[head][late] = accum_in[head][late] * decay[:1]

        def add(scores, late, rows):
            weights = jnp.exp2((scores - peak[head][late][:1]) * SCALE)
            total[head][late] += folded(weights, jnp.sum)
            accum[head][late] += lax.dot_general(
                kv[rows, pl.ds((KV_HEADS + head) * HEAD, HEAD)],
                weights.astype(BF16),
                (((0,), (0,)), ((), ())),
                preferred_element_type=F32,
            )

        def step_a(index):
            add(scores_a[slot(head), a_rows(index), :], 1, a_rows(index))

        def step_b(index):
            late, _, rows = b_unit(index)
            add(scores_b[slot(head), b_rows(index), :], late, rows)

        yield from each(len(a_steps), step_a)
        yield from each(b_units, step_b)
        if last:
            for late in range(2):
                blended = accum[head][late] * (1.0 / jnp.sum(total[head][late], axis=0, keepdims=True))
                blended = blended.astype(BF16).T
                for g in range(GROUP):
                    result[head, late, :, g * HEAD : (g + 1) * HEAD] = blended[g * half : (g + 1) * half]
                columns = pl.ds(head * GROUP * HEAD, GROUP * HEAD)
                put = pltpu.make_async_copy(
                    result.at[head, late], out.at[query_rows[late], columns], put_sems.at[2 * head + late]
                )
                put.start()
                puts.append(put)
                yield

    puts = []
    if scores_a.shape[0] == heads:
        order = [step(head) for step in (find_scores, blend) for head in range(heads)]
    else:
        order = [step(head) for head in range(heads) for step in (find_scores, blend)]
    for steps in order:
        for _ in steps:
            pass
    for put in puts:
        put.wait()


def attend(devices, offsets, spans, queries, pieces, state=(), last=True):
    rows = queries.shape[0]
    half = rows // 2
    lanes = GROUP * half
    blocks = sum(len(group) for group in offsets)
    part_rows = -(-blocks // UNIT) * UNIT * half
    b_rows = unit_count(blocks, offsets[0][0] == 0) * UNIT * half
    shapes = [(2, 8, lanes)] * (2 * KV_HEADS) + [(2, HEAD, lanes)] * KV_HEADS
    states = [VMEM(shape, F32) for shape in shapes]
    relayed = len(offsets) == blocks
    slots = KV_HEADS if relayed else 1
    if last:
        out_shape, out_specs = jax.ShapeDtypeStruct((rows, HEADS * HEAD), BF16), placed(pl.ANY)
    else:
        out_shape, out_specs = [jax.ShapeDtypeStruct(shape, F32) for shape in shapes], [placed(VMEM)] * len(shapes)
    return pl.pallas_call(
        functools.partial(attention_kernel, devices, offsets, not state, last),
        out_shape=out_shape,
        in_specs=[placed(SMEM), placed(VMEM)]
        + [placed(VMEM if relayed else pl.ANY)] * len(pieces)
        + [placed(VMEM)] * len(state),
        out_specs=out_specs,
        scratch_shapes=(states if last else [])
        + [
            VMEM((2 * part_rows, pieces[0].shape[1]), BF16),
            VMEM((slots, blocks * half, lanes), F32),
            VMEM((slots, b_rows, lanes), F32),
            VMEM((KV_HEADS, 2, lanes, HEAD), BF16),
            VMEM((KV_HEADS, 2, half, GROUP * HEAD) if last else (8, HEAD), BF16),
            DMA,
            DMA((2 * KV_HEADS,)),
        ],
        compiler_params=pltpu.CompilerParams(vmem_limit_bytes=(20 if relayed else 63) << 20),
        cost_estimate=pl.CostEstimate(
            flops=8 * rows * rows * blocks * HEADS * HEAD // 2, bytes_accessed=2 * rows * HEADS * HEAD, transcendentals=0
        ),
        name="attention",
    )(spans, queries, *pieces, *state)


def body(hidden_in, span_order, norm_gain, w_query, w_key, w_value, query_gain, key_gain):
    rows, width = hidden_in.shape
    half = rows // 2
    devices = lax.axis_size("ctx")
    kv_width = 2 * KV_HEADS * HEAD
    steps = table(half, 2 * devices)
    span_order = span_order.T

    shared_width = width + 6 * HEAD
    shared, kv = pl.pallas_call(
        key_value_kernel,
        out_shape=(jax.ShapeDtypeStruct((rows, shared_width), BF16), jax.ShapeDtypeStruct((rows, kv_width), BF16)),
        in_specs=[placed(pl.ANY)] * 8,
        out_specs=[placed(pl.ANY), placed(VMEM)],
        scratch_shapes=[
            SMEM(span_order.shape, jnp.int32),
            VMEM((rows, width), BF16),
            VMEM((1, width), F32),
            VMEM(w_key.shape, BF16),
            VMEM(w_value.shape, BF16),
            VMEM((1, HEAD), F32),
            VMEM((1, HEAD), F32),
            VMEM(steps.shape, F32),
            VMEM((rows, shared_width), BF16),
            VMEM((rows, 2 * HEAD), F32),
            DMA((8,)),
        ],
        compiler_params=pltpu.CompilerParams(vmem_limit_bytes=63 << 20),
        name="key_value",
    )(
        span_order,
        hidden_in,
        norm_gain.reshape(1, width),
        w_key,
        w_value,
        key_gain.reshape(1, HEAD),
        query_gain.reshape(1, HEAD),
        steps,
    )

    tiles = HEADS * HEAD // TILE
    queries = pl.pallas_call(
        query_kernel,
        out_shape=jax.ShapeDtypeStruct((rows, HEADS * HEAD), BF16),
        in_specs=[placed(pl.ANY)] * 2,
        out_specs=placed(VMEM),
        scratch_shapes=[
            VMEM((rows, shared_width), BF16),
            VMEM((tiles, width, TILE), BF16),
            VMEM((2, rows, TILE), F32),
            DMA((1 + tiles,)),
        ],
        compiler_params=pltpu.CompilerParams(vmem_limit_bytes=53 << 20),
        cost_estimate=pl.CostEstimate(
            flops=2 * rows * width * HEADS * HEAD, bytes_accessed=2 * width * HEADS * HEAD, transcendentals=0
        ),
        name="query",
    )(shared, w_query)

    far = devices // 2
    if devices > 16:
        held, count = kv, 1
        while count < far:
            held = jnp.concatenate([held, partner(held, count)])
            count *= 2
        pieces, offsets = [held, partner(held, far)], [list(range(far)), list(range(far, devices))]
        return attend(devices, offsets, span_order, queries, pieces)

    def cores(pieces):
        for offset in list(pieces):
            pieces[offset + 1] = partner(pieces[offset], 1)
        return [[offset] for offset in pieces], list(pieces.values())

    near = range(2, far, 2)
    pieces = {0: kv, far: partner(kv, far)}
    for offset in near:
        pieces[offset] = partner(kv, offset)
    relayed = {}
    for offset in near:
        relayed[far + offset] = partner(pieces[far], offset)
    offsets, pieces = cores(pieces)
    state = attend(devices, offsets, span_order, queries, pieces, last=False)
    offsets, pieces = cores(relayed)
    return attend(devices, offsets, span_order, queries, pieces, state)


def solution(mesh):
    in_specs = (P(("groups", "ctx"), None), P("groups", None), P(), P(), P(), P(), P(), P())
    out_specs = P(("groups", "ctx"), None)
    return jax.shard_map(body, mesh=mesh, in_specs=in_specs, out_specs=out_specs, check_vma=False)
```
